32 devices in a mesh: row: 4 (over z), col: 8 (over y, x, core).
Axes of the slice: x: 2, y: 2, z: 4, core: 2. Of those that a mesh axis runs over, the one named last changes fastest.
Arguments:
- hessian: float32 [16384, 4, 8, 512], P('row', None, 'col'), may hold values from -1 to 16, as said below
- weights: bfloat16 [512, 16384], P('col', 'row'), may hold values from -6 to 6
- codes: int32 [512, 8192], P('col', 'row'), may hold values from 0 to 255
- tile_map: int32 [32, 64], P('col', 'row'), may hold values from 0 to 511
- codebooks: float32 [512, 2, 256], replicated, may hold values from -6 to 6
Outputs:
- adjusted_codebooks: float32 [512, 2, 256], replicated
The draws below stay inside these ranges and needn't reach their ends.
Inputs may be any that keep to these rules, and one draw needn't show every extreme that they name: `hessian`: H is symmetric with a dominant positive diagonal.
All inputs are finite; a program needn't handle non-finite values.
Results may differ from the reference program's by a relative error of at most 0.0003.
Values sent between devices are 32-bit elements; how exact they have to be, the bound alone decides.
A program may use at most 192 MiB of HBM per device.

```python
import math
import jax
import jax.numpy as jnp
from jax import lax

D = 16384
R = 512
CODES = 256
NB = 512
TILE_ROWS = 16
TILE_COLS = 256
STEPS = 2
N_ROW = 4
N_COL = 8


def draw_hessian(key, part):
    base_key = jax.random.fold_in(key, 23)
    scale_key, noise_key, diag_key = jax.random.split(base_key, 3)
    scales = jnp.exp(jax.random.uniform(scale_key, (D,), jnp.float32, math.log(0.5), math.log(2.0)))
    noise = jnp.clip(jax.random.normal(noise_key, (D, D), jnp.float32), -5.0, 5.0)
    damping = jax.random.uniform(diag_key, (D,), jnp.float32, 1.0, 1.5)
    symmetric = (noise + noise.T) * (0.3 / math.sqrt(2.0 * D))
    eye = (lax.broadcasted_iota(jnp.int32, (D, D), 0) == lax.broadcasted_iota(jnp.int32, (D, D), 1)).astype(jnp.float32)
    inner = symmetric + eye * damping[:, None]
    outer = scales[:, None] * scales[None, :]
    values = outer * inner
    return values.reshape(D, N_ROW, N_COL, D // (N_ROW * N_COL))


def touch_ends(result, stream_key, low, top_value):
    longest = result.shape.index(max(result.shape))
    spots = []
    for shift in (0, 1):
        where = [jax.random.randint(jax.random.fold_in(stream_key, axis), (), 0, length) for axis, length in enumerate(result.shape)]
        where[longest] = (where[longest] + shift) % result.shape[longest]
        spots.append(tuple(where))
    return result.at[spots[0]].set(low).at[spots[1]].set(top_value)


def block_levels(rng, dims, cuts, least, largest):
    def one(dim, blocks):
        steps = jax.random.uniform(jax.random.fold_in(jax.random.fold_in(rng, 6), dim), (blocks,), jnp.float32, least / len(cuts), largest / len(cuts))
        return jnp.repeat(jnp.exp(steps), dims[dim] // blocks).reshape((-1,) + (1,) * (len(dims) - dim - 1))

    gain = one(*cuts[0])
    for cut in cuts[1:]:
        gain = gain * one(*cut)
    return gain


def bell_draw(rng, dims, scale, most, shards=(), held_as=jnp.bfloat16):
    drawn = jax.random.normal(rng, dims, jnp.float32) * scale
    if len(shards) > 0:
        drawn = block_levels(rng, dims, shards, -0.22, 0.18) * drawn
    return jnp.clip(drawn, min=-most, max=most).astype(held_as)


def setup_inputs(seed: int = 0) -> dict:
    streams_of = jax.random.split(jax.random.key(seed), 6)
    hessian = draw_hessian(jax.random.fold_in(streams_of[5], 71), 0)
    weights = bell_draw(streams_of[1], (R, D), 1.0, 6.0, ((0, 8), (1, 4)))
    codes = touch_ends(jax.random.randint(streams_of[2], (R, D // 2), 0, CODES), jax.random.fold_in(streams_of[2], 1), 0, CODES - 1).astype(jnp.int32)
    tile_map = touch_ends(jax.random.randint(streams_of[3], (R // TILE_ROWS, D // TILE_COLS), 0, NB), jax.random.fold_in(streams_of[3], 1), 0, NB - 1).astype(jnp.int32)
    codebooks = bell_draw(streams_of[4], (NB, 2, CODES), 1.0, 6.0, (), jnp.float32)
    return {"hessian": hessian, "weights": weights, "codes": codes, "tile_map": tile_map, "codebooks": codebooks}


learn_rate = 0.01


def book_index(tile_map):
    spread = jnp.repeat(tile_map, TILE_ROWS, axis=0)
    return jnp.repeat(spread, TILE_COLS // 2, axis=1)


def reference(hessian, weights, codes, tile_map, codebooks):
    full_hessian = hessian.reshape(D, D)
    flat_index = (book_index(tile_map) * CODES + codes).astype(jnp.int32)
    for iteration in range(STEPS):
        table_even = codebooks[:, 0, :].reshape(-1)
        table_odd = codebooks[:, 1, :].reshape(-1)
        rebuilt = jnp.stack([table_even[flat_index], table_odd[flat_index]], axis=-1).reshape(R, D)
        error = rebuilt - weights.astype(jnp.float32)
        weight_grad = 2.0 * jnp.dot(error, full_hessian, precision=lax.Precision.HIGHEST)
        grad_even = jax.ops.segment_sum(weight_grad[:, 0::2].reshape(-1), flat_index.reshape(-1), NB * CODES)
        grad_odd = jax.ops.segment_sum(weight_grad[:, 1::2].reshape(-1), flat_index.reshape(-1), NB * CODES)
        book_grad = jnp.stack([grad_even.reshape(NB, CODES), grad_odd.reshape(NB, CODES)], axis=1)
        codebooks = codebooks - learn_rate * book_grad
    return codebooks
```

```python
import functools

import jax
import jax.numpy as jnp
from jax import lax
from jax.experimental import pallas as pl
from jax.experimental.pallas import tpu as pltpu
from jax.sharding import PartitionSpec as P

TILE_ROWS = 16
TILE_COLS = 256
STEPS = 2
LANES = 128
HALF = TILE_COLS // 2

learn_rate = 0.01
MESH = pl.DeviceIdType.MESH
NT = (((1,), (1,)), ((), ()))


def split_kernel(hessian_ref, high_ref, low_ref):
    rows, width = high_ref.shape
    stride = width // LANES
    for k in range(stride):
        x = hessian_ref[pl.ds(k, rows, stride=stride), :]
        high = x.astype(jnp.bfloat16)
        high_ref[:, k * LANES : (k + 1) * LANES] = high
        low_ref[:, k * LANES : (k + 1) * LANES] = (x - high.astype(jnp.float32)).astype(jnp.bfloat16)


def split_hessian(hessian):
    rows = hessian.shape[0]
    width = hessian.shape[1] * hessian.shape[2] * hessian.shape[3]
    stride = width // LANES
    block = min(rows, 256)
    part = jax.ShapeDtypeStruct((rows, width), jnp.bfloat16)
    spec = pl.BlockSpec((block, width), lambda i: (i, 0))
    return pl.pallas_call(
        split_kernel,
        grid=(rows // block,),
        in_specs=[pl.BlockSpec((block * stride, LANES), lambda i: (i, 0))],
        out_specs=[spec, spec],
        out_shape=[part, part],
        cost_estimate=pl.CostEstimate(flops=rows * width * 4, bytes_accessed=rows * width * 8, transcendentals=0),
        name="split_hessian",
    )(hessian.reshape(rows * stride, LANES))


def pick(table, index):
    return jnp.take_along_axis(table, index, axis=1, mode="promise_in_bounds")


def error_kernel(map_ref, codes_ref, weights_ref, books_ref, error_ref):
    tiles_down, tiles_across = map_ref.shape
    shape = (TILE_ROWS, LANES)
    lane = lax.broadcasted_iota(jnp.int32, shape, 1)
    odd = (lane & 1) == 1

    def tile(t, carry):
        i, j = t // tiles_across, t % tiles_across
        table = books_ref[map_ref[i, j]]
        rows = pl.ds(pl.multiple_of(i * TILE_ROWS, TILE_ROWS), TILE_ROWS)
        codes = codes_ref[rows, pl.ds(pl.multiple_of(j * HALF, HALF), HALF)]
        tables = [jnp.broadcast_to(table[n : n + 1, :], shape) for n in range(4)]
        for half in range(2):
            code = pick(codes, (lane >> 1) + half * (LANES // 2))
            index = code & (LANES - 1)
            upper = code >= LANES
            near = jnp.where(odd, pick(tables[1], index), pick(tables[0], index))
            far = jnp.where(odd, pick(tables[3], index), pick(tables[2], index))
            columns = pl.ds(pl.multiple_of(j * TILE_COLS + half * LANES, LANES), LANES)
            error_ref[rows, columns] = jnp.where(upper, far, near) - weights_ref[rows, columns].astype(jnp.float32)
        return carry

    lax.fori_loop(0, tiles_down * tiles_across, tile, 0, unroll=2)


VMEM = pl.BlockSpec(memory_space=pltpu.VMEM)
SMEM = pl.BlockSpec(memory_space=pltpu.SMEM)


def errors(tile_map, codes, weights, books):
    return pl.pallas_call(
        error_kernel,
        in_specs=[SMEM, VMEM, VMEM, VMEM],
        out_specs=VMEM,
        out_shape=jax.ShapeDtypeStruct(weights.shape, jnp.float32),
        name="errors",
    )(tile_map, codes, weights, books.reshape(-1, 4, LANES))


def product_kernel(error_ref, high_ref, low_ref, out_ref, error_high, error_low):
    @pl.when(pl.program_id(0) == 0)
    def _():
        x = error_ref[...]
        high = x.astype(jnp.bfloat16)
        error_high[...] = high
        error_low[...] = (x - high.astype(jnp.float32)).astype(jnp.bfloat16)

    dot = functools.partial(lax.dot_general, dimension_numbers=NT, preferred_element_type=jnp.float32)
    total = dot(error_high[...], low_ref[...]) + dot(error_low[...], high_ref[...])
    out_ref[...] = total + dot(error_high[...], high_ref[...])


def product(error, high, low):
    m, k = error.shape
    n = high.shape[0]
    block = min(n, 512)
    spec = pl.BlockSpec((block, k), lambda i: (i, 0))
    return pl.pallas_call(
        product_kernel,
        grid=(n // block,),
        in_specs=[pl.BlockSpec((m, k), lambda i: (0, 0)), spec, spec],
        out_specs=pl.BlockSpec((m, block), lambda i: (0, i)),
        out_shape=jax.ShapeDtypeStruct((m, n), jnp.float32),
        scratch_shapes=[pltpu.VMEM((m, k), jnp.bfloat16), pltpu.VMEM((m, k), jnp.bfloat16)],
        cost_estimate=pl.CostEstimate(flops=6 * m * n * k, bytes_accessed=4 * n * k + 4 * m * (n + k), transcendentals=0),
        name="product",
    )(error, high, low)


def scatter_kernel(map_ref, codes_ref, grad_ref, books_ref):
    tiles_down, tiles_across = map_ref.shape
    shape = (TILE_ROWS, LANES)
    lane = lax.broadcasted_iota(jnp.int32, shape, 1)
    first = lane < LANES // 2
    even_index = (2 * lane) & (LANES - 1)
    line = lax.broadcasted_iota(jnp.int32, (8, LANES), 0)
    is_odd = (line & 1) == 1
    is_upper = (line & 2) == 2
    is_low = lax.broadcasted_iota(jnp.int32, (8, HALF * TILE_ROWS), 0) >= 4
    entry = lax.broadcasted_iota(jnp.int32, (LANES, LANES), 0)
    books_ref[...] = jnp.zeros_like(books_ref)

    def tile(t, carry):
        i, j = t // tiles_across, t % tiles_across
        rows = pl.ds(pl.multiple_of(i * TILE_ROWS, TILE_ROWS), TILE_ROWS)
        codes = codes_ref[rows, pl.ds(pl.multiple_of(j * HALF, HALF), HALF)]
        left = grad_ref[rows, pl.ds(pl.multiple_of(j * TILE_COLS, LANES), LANES)]
        right = grad_ref[rows, pl.ds(pl.multiple_of(j * TILE_COLS + LANES, LANES), LANES)]
        even = jnp.where(first, pick(left, even_index), pick(right, even_index))
        odd = jnp.where(first, pick(left, even_index + 1), pick(right, even_index + 1))
        index = codes & (LANES - 1)
        upper = jnp.where(codes >= LANES, 1, 0)
        values, hots = [], []
        for n in range(TILE_ROWS):
            value = jnp.where(is_odd, odd[n : n + 1, :], even[n : n + 1, :])
            fits = is_upper == (jnp.broadcast_to(upper[n : n + 1, :], (8, LANES)) == 1)
            values.append(jnp.where(fits, value, 0.0))
            hots.append(jnp.where(entry == index[n : n + 1, :], 1.0, 0.0).astype(jnp.bfloat16))
        value = jnp.concatenate(values, axis=1)
        high = value.astype(jnp.bfloat16).astype(jnp.float32)
        parts = jnp.where(is_low, value - high, high).astype(jnp.bfloat16)
        sums = lax.dot_general(parts, jnp.concatenate(hots, axis=1), NT, preferred_element_type=jnp.float32)
        book = map_ref[i, j]
        books_ref[book] += sums[0:4, :] + sums[4:8, :]
        return carry

    lax.fori_loop(0, tiles_down * tiles_across, tile, 0)


def scatter(tile_map, codes, grad, books):
    total = pl.pallas_call(
        scatter_kernel,
        in_specs=[SMEM, VMEM, VMEM],
        out_specs=VMEM,
        out_shape=jax.ShapeDtypeStruct((books.shape[0] // 4, 4, LANES), jnp.float32),
        name="scatter",
    )(tile_map, codes, grad)
    return total.reshape(books.shape)


def update_kernel(n_row, n_col, grad_ref, books_ref, out_ref, col_in, row_sum, row_in, col_send, col_recv, row_send, row_recv, row_send2, row_recv2, col_send2, col_recv2):
    r, c = lax.axis_index("row"), lax.axis_index("col")
    wide = grad_ref.shape[0] // n_col
    thin = wide // n_row
    cols = [lax.rem(c + d, n_col) for d in range(n_col)]
    rows = [lax.rem(r + d, n_row) for d in range(n_row)]

    barrier = pltpu.get_barrier_semaphore()
    for d in range(1, n_col):
        pl.semaphore_signal(barrier, inc=1, device_id=(r, cols[d]), device_id_type=MESH)
    for d in range(1, n_row):
        pl.semaphore_signal(barrier, inc=1, device_id=(rows[d], c), device_id_type=MESH)
    pl.semaphore_wait(barrier, n_col + n_row - 2)

    def piece(index, size):
        return pl.ds(pl.multiple_of(index * size, size), size)

    def send(src, dst, sends, recvs, d, device):
        copy = pltpu.make_async_remote_copy(
            src_ref=src, dst_ref=dst, send_sem=sends.at[d], recv_sem=recvs.at[d], device_id=device, device_id_type=MESH
        )
        copy.start()
        return copy

    first = [
        send(grad_ref.at[piece(cols[d], wide)], col_in.at[d], col_send, col_recv, d, (r, cols[d])) for d in range(1, n_col)
    ]
    total = grad_ref[piece(c, wide), :]
    for d, copy in enumerate(first, 1):
        copy.wait_recv()
        total = total + col_in[d]
    row_sum[...] = total
    second = [
        send(row_sum.at[piece(rows[d], thin)], row_in.at[d], row_send, row_recv, d, (rows[d], c)) for d in range(1, n_row)
    ]
    total = row_sum[piece(r, thin), :]
    for d, copy in enumerate(second, 1):
        copy.wait_recv()
        total = total + row_in[d]
    mine = piece(c * n_row + r, thin)
    out_ref[mine, :] = books_ref[mine, :] - learn_rate * (2.0 * total)
    third = [send(out_ref.at[mine], out_ref.at[mine], row_send2, row_recv2, d, (rows[d], c)) for d in range(1, n_row)]
    for copy in third:
        copy.wait_recv()
    whole = piece(c, wide)
    fourth = [send(out_ref.at[whole], out_ref.at[whole], col_send2, col_recv2, d, (r, cols[d])) for d in range(1, n_col)]
    for copy in fourth:
        copy.wait_recv()
    for copy in first + second + third + fourth:
        copy.wait_send()


def update(n_row, n_col, grad, books):
    wide = books.shape[0] // n_col
    thin = wide // n_row
    dma = pltpu.SemaphoreType.DMA
    return pl.pallas_call(
        functools.partial(update_kernel, n_row, n_col),
        in_specs=[VMEM, VMEM],
        out_specs=VMEM,
        out_shape=jax.ShapeDtypeStruct(books.shape, jnp.float32),
        scratch_shapes=[
            pltpu.VMEM((n_col, wide, LANES), jnp.float32),
            pltpu.VMEM((wide, LANES), jnp.float32),
            pltpu.VMEM((n_row, thin, LANES), jnp.float32),
            dma((n_col,)),
            dma((n_col,)),
            dma((n_row,)),
            dma((n_row,)),
            dma((n_row,)),
            dma((n_row,)),
            dma((n_col,)),
            dma((n_col,)),
        ],
        compiler_params=pltpu.CompilerParams(collective_id=0, has_side_effects=True),
        name="update",
    )(grad, books)


def per_device(n_row, n_col, hessian, weights, codes, tile_map, codebooks):
    count, parts, entries = codebooks.shape
    books = codebooks.reshape(count, parts, entries // LANES, LANES).transpose(0, 2, 1, 3).reshape(-1, LANES)
    high, low = split_hessian(hessian)
    for step in range(STEPS):
        error = errors(tile_map, codes, weights, books)
        piece = lax.all_to_all(error, "col", split_axis=1, concat_axis=0, tiled=True)
        spread = lax.all_gather(piece, "row", axis=1, tiled=True)
        partial = product(spread, high, low)
        grad = lax.psum_scatter(partial, "col", scatter_dimension=0, tiled=True)
        books = update(n_row, n_col, scatter(tile_map, codes, grad, books), books)
    return books.reshape(count, entries // LANES, parts, LANES).transpose(0, 2, 1, 3).reshape(codebooks.shape)


def solution(mesh):
    placed = (P("row", None, "col", None), P("col", "row"), P("col", "row"), P("col", "row"), P())
    body = functools.partial(per_device, mesh.shape["row"], mesh.shape["col"])
    return jax.shard_map(body, mesh=mesh, in_specs=placed, out_specs=P(), check_vma=False)
```

```python
import functools

import jax
import jax.numpy as jnp
from jax import lax
from jax.experimental import pallas as pl
from jax.experimental.pallas import tpu as pltpu
from jax.sharding import PartitionSpec as P

TILE_ROWS = 16
TILE_COLS = 256
STEPS = 2
LANES = 128
HALF = TILE_COLS // 2

learn_rate = 0.01
MESH = pl.DeviceIdType.MESH
NT = (((1,), (1,)), ((), ()))


def split_kernel(hessian_ref, high_ref, low_ref):
    rows, width = high_ref.shape
    stride = width // LANES
    for k in range(stride):
        x = hessian_ref[pl.ds(k, rows, stride=stride), :]
        high = x.astype(jnp.bfloat16)
        high_ref[:, k * LANES : (k + 1) * LANES] = high
        low_ref[:, k * LANES : (k + 1) * LANES] = (x - high.astype(jnp.float32)).astype(jnp.bfloat16)


def split_hessian(hessian):
    rows = hessian.shape[0]
    width = hessian.shape[1] * hessian.shape[2] * hessian.shape[3]
    stride = width // LANES
    block = min(rows, 256)
    part = jax.ShapeDtypeStruct((rows, width), jnp.bfloat16)
    spec = pl.BlockSpec((block, width), lambda i: (i, 0))
    return pl.pallas_call(
        split_kernel,
        grid=(rows // block,),
        in_specs=[pl.BlockSpec((block * stride, LANES), lambda i: (i, 0))],
        out_specs=[spec, spec],
        out_shape=[part, part],
        cost_estimate=pl.CostEstimate(flops=rows * width * 4, bytes_accessed=rows * width * 8, transcendentals=0),
        name="split_hessian",
    )(hessian.reshape(rows * stride, LANES))


def pick(table, index):
    return jnp.take_along_axis(table, index, axis=1, mode="promise_in_bounds")


def error_kernel(map_ref, codes_ref, weights_ref, books_ref, error_ref):
    tiles_down, tiles_across = map_ref.shape
    shape = (TILE_ROWS, LANES)
    lane = lax.broadcasted_iota(jnp.int32, shape, 1)
    odd = (lane & 1) == 1

    def tile(t, carry):
        i, j = t // tiles_across, t % tiles_across
        table = books_ref[map_ref[i, j]]
        rows = pl.ds(pl.multiple_of(i * TILE_ROWS, TILE_ROWS), TILE_ROWS)
        codes = codes_ref[rows, pl.ds(pl.multiple_of(j * HALF, HALF), HALF)]
        tables = [jnp.broadcast_to(table[n : n + 1, :], shape) for n in range(4)]
        for half in range(2):
            code = pick(codes, (lane >> 1) + half * (LANES // 2))
            index = code & (LANES - 1)
            upper = code >= LANES
            near = jnp.where(odd, pick(tables[1], index), pick(tables[0], index))
            far = jnp.where(odd, pick(tables[3], index), pick(tables[2], index))
            columns = pl.ds(pl.multiple_of(j * TILE_COLS + half * LANES, LANES), LANES)
            error_ref[rows, columns] = jnp.where(upper, far, near) - weights_ref[rows, columns].astype(jnp.float32)
        return carry

    lax.fori_loop(0, tiles_down * tiles_across, tile, 0, unroll=2)


VMEM = pl.BlockSpec(memory_space=pltpu.VMEM)
SMEM = pl.BlockSpec(memory_space=pltpu.SMEM)


def errors(tile_map, codes, weights, books):
    return pl.pallas_call(
        error_kernel,
        in_specs=[SMEM, VMEM, VMEM, VMEM],
        out_specs=VMEM,
        out_shape=jax.ShapeDtypeStruct(weights.shape, jnp.float32),
        name="errors",
    )(tile_map, codes, weights, books.reshape(-1, 4, LANES))


def product_kernel(chunks, error_ref, high_ref, low_ref, out_ref, error_high, error_low, made, pair_in, pair_sum, chip_in, pair_send, pair_recv, chip_send, chip_recv):
    n = pl.program_id(0)
    r, c = lax.axis_index("row"), lax.axis_index("col")
    chips = made.shape[1]
    block = made.shape[4]
    chip, core = c // 2, lax.rem(c, 2)
    others = [lax.rem(chip + d, chips) for d in range(chips)]

    @pl.when(n == 0)
    def _():
        barrier = pltpu.get_barrier_semaphore()
        pl.semaphore_signal(barrier, inc=1, device_id=(r, chip * 2 + 1 - core), device_id_type=MESH)
        for d in range(1, chips):
            pl.semaphore_signal(barrier, inc=1, device_id=(r, others[d] * 2 + core), device_id_type=MESH)
        x = error_ref[...]
        high = x.astype(jnp.bfloat16)
        error_high[...] = high
        error_low[...] = (x - high.astype(jnp.float32)).astype(jnp.bfloat16)
        pl.semaphore_wait(barrier, chips)

    def to_pair(k):
        return pltpu.make_async_remote_copy(
            src_ref=made.at[k, :, 1 - core],
            dst_ref=pair_in.at[k],
            send_sem=pair_send.at[k],
            recv_sem=pair_recv.at[k],
            device_id=(r, chip * 2 + 1 - core),
            device_id_type=MESH,
        )

    def to_chip(k, d):
        return pltpu.make_async_remote_copy(
            src_ref=pair_sum.at[k, others[d]],
            dst_ref=chip_in.at[d - 1, k],
            send_sem=chip_send.at[d - 1, k],
            recv_sem=chip_recv.at[d - 1, k],
            device_id=(r, others[d] * 2 + core),
            device_id_type=MESH,
        )

    def add_pair(k):
        to_pair(k).wait_recv()
        pair_sum[k] = made[k, :, core] + pair_in[k]
        for d in range(1, chips):
            to_chip(k, d).start()

    dot = functools.partial(lax.dot_general, dimension_numbers=NT, preferred_element_type=jnp.float32)
    total = dot(error_high[...], low_ref[...]) + dot(error_low[...], high_ref[...])
    total = total + dot(error_high[...], high_ref[...])
    made[n] = total.reshape(made.shape[1:])
    to_pair(n).start()

    @pl.when(n > 0)
    def _():
        add_pair(n - 1)

    @pl.when(n == chunks - 1)
    def _():
        add_pair(n)

        def finish(k, carry):
            total = pair_sum[k, chip]
            for d in range(1, chips):
                to_chip(k, d).wait_recv()
                total = total + chip_in[d - 1, k]
            out_ref[:, pl.ds(pl.multiple_of(k * block, block), block)] = total
            to_pair(k).wait_send()
            for d in range(1, chips):
                to_chip(k, d).wait_send()
            return carry

        lax.fori_loop(0, chunks, finish, 0)


def product(n_col, error, high, low):
    m, k = error.shape
    n = high.shape[0]
    block = min(n, 512)
    chunks = n // block
    chips = n_col // 2
    rows = m // n_col
    spec = pl.BlockSpec((block, k), lambda i: (i, 0))
    dma = pltpu.SemaphoreType.DMA
    return pl.pallas_call(
        functools.partial(product_kernel, chunks),
        grid=(chunks,),
        in_specs=[pl.BlockSpec((m, k), lambda i: (0, 0)), spec, spec],
        out_specs=pl.BlockSpec((rows, n), lambda i: (0, 0)),
        out_shape=jax.ShapeDtypeStruct((rows, n), jnp.float32),
        scratch_shapes=[
            pltpu.VMEM((m, k), jnp.bfloat16),
            pltpu.VMEM((m, k), jnp.bfloat16),
            pltpu.VMEM((chunks, chips, 2, rows, block), jnp.float32),
            pltpu.VMEM((chunks, chips, rows, block), jnp.float32),
            pltpu.VMEM((chunks, chips, rows, block), jnp.float32),
            pltpu.VMEM((chips - 1, chunks, rows, block), jnp.float32),
            dma((chunks,)),
            dma((chunks,)),
            dma((chips - 1, chunks)),
            dma((chips - 1, chunks)),
        ],
        compiler_params=pltpu.CompilerParams(collective_id=1, has_side_effects=True, vmem_limit_bytes=56 * 2**20),
        cost_estimate=pl.CostEstimate(flops=6 * m * n * k, bytes_accessed=4 * n * k + 4 * m * (n + k), transcendentals=0),
        name="product",
    )(error, high, low)


def scatter_kernel(map_ref, codes_ref, grad_ref, books_ref):
    tiles_down, tiles_across = map_ref.shape
    shape = (TILE_ROWS, LANES)
    lane = lax.broadcasted_iota(jnp.int32, shape, 1)
    first = lane < LANES // 2
    even_index = (2 * lane) & (LANES - 1)
    line = lax.broadcasted_iota(jnp.int32, (8, LANES), 0)
    is_odd = (line & 1) == 1
    is_upper = (line & 2) == 2
    is_low = lax.broadcasted_iota(jnp.int32, (8, HALF * TILE_ROWS), 0) >= 4
    entry = lax.broadcasted_iota(jnp.int32, (LANES, LANES), 0)
    books_ref[...] = jnp.zeros_like(books_ref)

    def tile(t, carry):
        i, j = t // tiles_across, t % tiles_across
        rows = pl.ds(pl.multiple_of(i * TILE_ROWS, TILE_ROWS), TILE_ROWS)
        codes = codes_ref[rows, pl.ds(pl.multiple_of(j * HALF, HALF), HALF)]
        left = grad_ref[rows, pl.ds(pl.multiple_of(j * TILE_COLS, LANES), LANES)]
        right = grad_ref[rows, pl.ds(pl.multiple_of(j * TILE_COLS + LANES, LANES), LANES)]
        even = jnp.where(first, pick(left, even_index), pick(right, even_index))
        odd = jnp.where(first, pick(left, even_index + 1), pick(right, even_index + 1))
        index = codes & (LANES - 1)
        upper = jnp.where(codes >= LANES, 1, 0)
        values, hots = [], []
        for n in range(TILE_ROWS):
            value = jnp.where(is_odd, odd[n : n + 1, :], even[n : n + 1, :])
            fits = is_upper == (jnp.broadcast_to(upper[n : n + 1, :], (8, LANES)) == 1)
            values.append(jnp.where(fits, value, 0.0))
            hots.append(jnp.where(entry == index[n : n + 1, :], 1.0, 0.0).astype(jnp.bfloat16))
        value = jnp.concatenate(values, axis=1)
        high = value.astype(jnp.bfloat16).astype(jnp.float32)
        parts = jnp.where(is_low, value - high, high).astype(jnp.bfloat16)
        sums = lax.dot_general(parts, jnp.concatenate(hots, axis=1), NT, preferred_element_type=jnp.float32)
        book = map_ref[i, j]
        books_ref[book] += sums[0:4, :] + sums[4:8, :]
        return carry

    lax.fori_loop(0, tiles_down * tiles_across, tile, 0)


def scatter(tile_map, codes, grad, books):
    total = pl.pallas_call(
        scatter_kernel,
        in_specs=[SMEM, VMEM, VMEM],
        out_specs=VMEM,
        out_shape=jax.ShapeDtypeStruct((books.shape[0] // 4, 4, LANES), jnp.float32),
        name="scatter",
    )(tile_map, codes, grad)
    return total.reshape(books.shape)


def update_kernel(n_row, n_col, grad_ref, books_ref, out_ref, col_in, row_sum, row_in, col_send, col_recv, row_send, row_recv, row_send2, row_recv2, col_send2, col_recv2):
    r, c = lax.axis_index("row"), lax.axis_index("col")
    wide = grad_ref.shape[0] // n_col
    thin = wide // n_row
    cols = [lax.rem(c + d, n_col) for d in range(n_col)]
    rows = [lax.rem(r + d, n_row) for d in range(n_row)]

    barrier = pltpu.get_barrier_semaphore()
    for d in range(1, n_col):
        pl.semaphore_signal(barrier, inc=1, device_id=(r, cols[d]), device_id_type=MESH)
    for d in range(1, n_row):
        pl.semaphore_signal(barrier, inc=1, device_id=(rows[d], c), device_id_type=MESH)
    pl.semaphore_wait(barrier, n_col + n_row - 2)

    def piece(index, size):
        return pl.ds(pl.multiple_of(index * size, size), size)

    def send(src, dst, sends, recvs, d, device):
        copy = pltpu.make_async_remote_copy(
            src_ref=src, dst_ref=dst, send_sem=sends.at[d], recv_sem=recvs.at[d], device_id=device, device_id_type=MESH
        )
        copy.start()
        return copy

    first = [
        send(grad_ref.at[piece(cols[d], wide)], col_in.at[d], col_send, col_recv, d, (r, cols[d])) for d in range(1, n_col)
    ]
    total = grad_ref[piece(c, wide), :]
    for d, copy in enumerate(first, 1):
        copy.wait_recv()
        total = total + col_in[d]
    row_sum[...] = total
    second = [
        send(row_sum.at[piece(rows[d], thin)], row_in.at[d], row_send, row_recv, d, (rows[d], c)) for d in range(1, n_row)
    ]
    total = row_sum[piece(r, thin), :]
    for d, copy in enumerate(second, 1):
        copy.wait_recv()
        total = total + row_in[d]
    mine = piece(c * n_row + r, thin)
    out_ref[mine, :] = books_ref[mine, :] - learn_rate * (2.0 * total)
    third = [send(out_ref.at[mine], out_ref.at[mine], row_send2, row_recv2, d, (rows[d], c)) for d in range(1, n_row)]
    for copy in third:
        copy.wait_recv()
    whole = piece(c, wide)
    fourth = [send(out_ref.at[whole], out_ref.at[whole], col_send2, col_recv2, d, (r, cols[d])) for d in range(1, n_col)]
    for copy in fourth:
        copy.wait_recv()
    for copy in first + second + third + fourth:
        copy.wait_send()


def update(n_row, n_col, grad, books):
    wide = books.shape[0] // n_col
    thin = wide // n_row
    dma = pltpu.SemaphoreType.DMA
    return pl.pallas_call(
        functools.partial(update_kernel, n_row, n_col),
        in_specs=[VMEM, VMEM],
        out_specs=VMEM,
        out_shape=jax.ShapeDtypeStruct(books.shape, jnp.float32),
        scratch_shapes=[
            pltpu.VMEM((n_col, wide, LANES), jnp.float32),
            pltpu.VMEM((wide, LANES), jnp.float32),
            pltpu.VMEM((n_row, thin, LANES), jnp.float32),
            dma((n_col,)),
            dma((n_col,)),
            dma((n_row,)),
            dma((n_row,)),
            dma((n_row,)),
            dma((n_row,)),
            dma((n_col,)),
            dma((n_col,)),
        ],
        compiler_params=pltpu.CompilerParams(collective_id=0, has_side_effects=True),
        name="update",
    )(grad, books)


def per_device(n_row, n_col, hessian, weights, codes, tile_map, codebooks):
    count, parts, entries = codebooks.shape
    books = codebooks.reshape(count, parts, entries // LANES, LANES).transpose(0, 2, 1, 3).reshape(-1, LANES)
    high, low = split_hessian(hessian)
    for step in range(STEPS):
        error = errors(tile_map, codes, weights, books)
        piece = lax.all_to_all(error, "col", split_axis=1, concat_axis=0, tiled=True)
        spread = lax.all_gather(piece, "row", axis=1, tiled=True)
        grad = product(n_col, spread, high, low)
        books = update(n_row, n_col, scatter(tile_map, codes, grad, books), books)
    return books.reshape(count, entries // LANES, parts, LANES).transpose(0, 2, 1, 3).reshape(codebooks.shape)


def solution(mesh):
    placed = (P("row", None, "col", None), P("col", "row"), P("col", "row"), P("col", "row"), P())
    body = functools.partial(per_device, mesh.shape["row"], mesh.shape["col"])
    return jax.shard_map(body, mesh=mesh, in_specs=placed, out_specs=P(), check_vma=False)
```

```python
import functools

import jax
import jax.numpy as jnp
from jax import lax
from jax.experimental import pallas as pl
from jax.experimental.pallas import tpu as pltpu
from jax.sharding import PartitionSpec as P

TILE_ROWS = 16
TILE_COLS = 256
STEPS = 2
LANES = 128
HALF = TILE_COLS // 2

learn_rate = 0.01
MESH = pl.DeviceIdType.MESH
NT = (((1,), (1,)), ((), ()))


def split_kernel(hessian_ref, high_ref, low_ref):
    rows, width = high_ref.shape
    stride = width // LANES
    for k in range(stride):
        x = hessian_ref[pl.ds(k, rows, stride=stride), :]
        high = x.astype(jnp.bfloat16)
        high_ref[:, k * LANES : (k + 1) * LANES] = high
        low_ref[:, k * LANES : (k + 1) * LANES] = (x - high.astype(jnp.float32)).astype(jnp.bfloat16)


def split_hessian(hessian):
    rows = hessian.shape[0]
    width = hessian.shape[1] * hessian.shape[2] * hessian.shape[3]
    stride = width // LANES
    block = min(rows, 256)
    part = jax.ShapeDtypeStruct((rows, width), jnp.bfloat16)
    spec = pl.BlockSpec((block, width), lambda i: (i, 0))
    return pl.pallas_call(
        split_kernel,
        grid=(rows // block,),
        in_specs=[pl.BlockSpec((block * stride, LANES), lambda i: (i, 0))],
        out_specs=[spec, spec],
        out_shape=[part, part],
        cost_estimate=pl.CostEstimate(flops=rows * width * 4, bytes_accessed=rows * width * 8, transcendentals=0),
        name="split_hessian",
    )(hessian.reshape(rows * stride, LANES))


def pick(table, index):
    return jnp.take_along_axis(table, index, axis=1, mode="promise_in_bounds")


def lookup(table, code):
    index = code & (LANES - 1)
    upper = code >= LANES
    tables = [jnp.broadcast_to(table[n : n + 1, :], code.shape) for n in range(4)]
    even = jnp.where(upper, pick(tables[2], index), pick(tables[0], index))
    odd = jnp.where(upper, pick(tables[3], index), pick(tables[1], index))
    return even, odd


def error_kernel(map_ref, codes_ref, weights_ref, books_ref, error_ref):
    tiles_down, tiles_across = map_ref.shape
    lane = lax.broadcasted_iota(jnp.int32, (TILE_ROWS, LANES), 1)
    is_odd = (lane & 1) == 1

    def tile(t, carry):
        i, j = t // tiles_across, t % tiles_across
        rows = pl.ds(pl.multiple_of(i * TILE_ROWS, TILE_ROWS), TILE_ROWS)
        codes = codes_ref[rows, pl.ds(pl.multiple_of(j * HALF, HALF), HALF)]
        even, odd = lookup(books_ref[map_ref[i, j]], codes)
        for half in range(2):
            source = (lane >> 1) + half * (LANES // 2)
            value = jnp.where(is_odd, pick(odd, source), pick(even, source))
            columns = pl.ds(pl.multiple_of(j * TILE_COLS + half * LANES, LANES), LANES)
            error_ref[rows, columns] = value - weights_ref[rows, columns].astype(jnp.float32)
        return carry

    lax.fori_loop(0, tiles_down * tiles_across, tile, 0, unroll=4)


def shift_kernel(run, gap, col_ref, map_ref, codes_ref, error_ref, new_ref, old_ref, out_ref):
    rows_here, pairs = codes_ref.shape
    down, across = rows_here // TILE_ROWS, pairs // HALF
    top = pl.program_id(0) * down
    lane = lax.broadcasted_iota(jnp.int32, (TILE_ROWS, LANES), 1)
    is_odd = (lane & 1) == 1
    begin = col_ref[0] * run

    def table(i, column):
        place = (column // run) * gap + begin + column % run
        book = map_ref[top + i, place // TILE_COLS]
        return new_ref[book] - old_ref[book]

    def tile(t, carry):
        i, j = t // across, t % across
        rows = pl.ds(pl.multiple_of(i * TILE_ROWS, TILE_ROWS), TILE_ROWS)
        codes = codes_ref[rows, pl.ds(pl.multiple_of(j * HALF, HALF), HALF)]
        even, odd = lookup(table(i, j * TILE_COLS), codes)
        if run % TILE_COLS:
            even2, odd2 = lookup(table(i, j * TILE_COLS + LANES), codes)
            second = lane >= LANES // 2
            even, odd = jnp.where(second, even2, even), jnp.where(second, odd2, odd)
        for half in range(2):
            source = (lane >> 1) + half * (LANES // 2)
            value = jnp.where(is_odd, pick(odd, source), pick(even, source))
            columns = pl.ds(pl.multiple_of(j * TILE_COLS + half * LANES, LANES), LANES)
            out_ref[rows, columns] = error_ref[rows, columns] + value
        return carry

    lax.fori_loop(0, down * across, tile, 0, unroll=4)


def shift(run, gap, full_map, codes, error, new, old):
    m, k = error.shape
    block = min(m, 128)
    col = jnp.full((1,), lax.axis_index("col"), jnp.int32)
    books = pl.BlockSpec((new.shape[0] // 4, 4, LANES), lambda i: (0, 0, 0))
    spec = pl.BlockSpec((block, k), lambda i: (i, 0))
    return pl.pallas_call(
        functools.partial(shift_kernel, run, gap),
        grid=(m // block,),
        in_specs=[SMEM, SMEM, pl.BlockSpec((block, k // 2), lambda i: (i, 0)), spec, books, books],
        out_specs=spec,
        out_shape=jax.ShapeDtypeStruct((m, k), jnp.float32),
        name="shift",
    )(col, full_map, codes, error, new.reshape(-1, 4, LANES), old.reshape(-1, 4, LANES))


VMEM = pl.BlockSpec(memory_space=pltpu.VMEM)
SMEM = pl.BlockSpec(memory_space=pltpu.SMEM)


def errors(tile_map, codes, weights, books):
    return pl.pallas_call(
        error_kernel,
        in_specs=[SMEM, VMEM, VMEM, VMEM],
        out_specs=VMEM,
        out_shape=jax.ShapeDtypeStruct(weights.shape, jnp.float32),
        name="errors",
    )(tile_map, codes, weights, books.reshape(-1, 4, LANES))


def product_kernel(chunks, error_ref, high_ref, low_ref, out_ref, error_high, error_low, made, pair_in, pair_sum, chip_in, pair_send, pair_recv, chip_send, chip_recv):
    n = pl.program_id(0)
    r, c = lax.axis_index("row"), lax.axis_index("col")
    chips = made.shape[1]
    block = made.shape[4]
    chip, core = c // 2, lax.rem(c, 2)
    others = [lax.rem(chip + d, chips) for d in range(chips)]

    @pl.when(n == 0)
    def _():
        barrier = pltpu.get_barrier_semaphore()
        pl.semaphore_signal(barrier, inc=1, device_id=(r, chip * 2 + 1 - core), device_id_type=MESH)
        for d in range(1, chips):
            pl.semaphore_signal(barrier, inc=1, device_id=(r, others[d] * 2 + core), device_id_type=MESH)
        x = error_ref[...]
        high = x.astype(jnp.bfloat16)
        error_high[...] = high
        error_low[...] = (x - high.astype(jnp.float32)).astype(jnp.bfloat16)
        pl.semaphore_wait(barrier, chips)

    def to_pair(k):
        return pltpu.make_async_remote_copy(
            src_ref=made.at[k, :, 1 - core],
            dst_ref=pair_in.at[k],
            send_sem=pair_send.at[k],
            recv_sem=pair_recv.at[k],
            device_id=(r, chip * 2 + 1 - core),
            device_id_type=MESH,
        )

    def to_chip(k, d):
        return pltpu.make_async_remote_copy(
            src_ref=pair_sum.at[k, others[d]],
            dst_ref=chip_in.at[d - 1, k],
            send_sem=chip_send.at[d - 1, k],
            recv_sem=chip_recv.at[d - 1, k],
            device_id=(r, others[d] * 2 + core),
            device_id_type=MESH,
        )

    def add_pair(k):
        to_pair(k).wait_recv()
        pair_sum[k] = made[k, :, core] + pair_in[k]
        for d in range(1, chips):
            to_chip(k, d).start()

    dot = functools.partial(lax.dot_general, dimension_numbers=NT, preferred_element_type=jnp.float32)
    total = dot(error_high[...], low_ref[...]) + dot(error_low[...], high_ref[...])
    total = total + dot(error_high[...], high_ref[...])
    made[n] = total.reshape(made.shape[1:])
    to_pair(n).start()

    @pl.when(n > 0)
    def _():
        add_pair(n - 1)

    @pl.when(n == chunks - 1)
    def _():
        add_pair(n)

        def finish(k, carry):
            total = pair_sum[k, chip]
            for d in range(1, chips):
                to_chip(k, d).wait_recv()
                total = total + chip_in[d - 1, k]
            out_ref[:, pl.ds(pl.multiple_of(k * block, block), block)] = total
            to_pair(k).wait_send()
            for d in range(1, chips):
                to_chip(k, d).wait_send()
            return carry

        lax.fori_loop(0, chunks, finish, 0)


def product(n_col, error, high, low):
    m, k = error.shape
    n = high.shape[0]
    block = min(n, 512)
    chunks = n // block
    chips = n_col // 2
    rows = m // n_col
    spec = pl.BlockSpec((block, k), lambda i: (i, 0))
    dma = pltpu.SemaphoreType.DMA
    return pl.pallas_call(
        functools.partial(product_kernel, chunks),
        grid=(chunks,),
        in_specs=[pl.BlockSpec((m, k), lambda i: (0, 0)), spec, spec],
        out_specs=pl.BlockSpec((rows, n), lambda i: (0, 0)),
        out_shape=jax.ShapeDtypeStruct((rows, n), jnp.float32),
        scratch_shapes=[
            pltpu.VMEM((m, k), jnp.bfloat16),
            pltpu.VMEM((m, k), jnp.bfloat16),
            pltpu.VMEM((chunks, chips, 2, rows, block), jnp.float32),
            pltpu.VMEM((chunks, chips, rows, block), jnp.float32),
            pltpu.VMEM((chunks, chips, rows, block), jnp.float32),
            pltpu.VMEM((chips - 1, chunks, rows, block), jnp.float32),
            dma((chunks,)),
            dma((chunks,)),
            dma((chips - 1, chunks)),
            dma((chips - 1, chunks)),
        ],
        compiler_params=pltpu.CompilerParams(collective_id=1, has_side_effects=True, vmem_limit_bytes=56 * 2**20),
        cost_estimate=pl.CostEstimate(flops=6 * m * n * k, bytes_accessed=4 * n * k + 4 * m * (n + k), transcendentals=0),
        name="product",
    )(error, high, low)


def scatter_kernel(map_ref, codes_ref, grad_ref, books_ref):
    tiles_down, tiles_across = map_ref.shape
    shape = (TILE_ROWS, LANES)
    lane = lax.broadcasted_iota(jnp.int32, shape, 1)
    first = lane < LANES // 2
    even_index = (2 * lane) & (LANES - 1)
    line = lax.broadcasted_iota(jnp.int32, (8, LANES), 0)
    is_odd = (line & 1) == 1
    is_upper = (line & 2) == 2
    is_low = lax.broadcasted_iota(jnp.int32, (8, HALF * TILE_ROWS), 0) >= 4
    entry = lax.broadcasted_iota(jnp.int32, (LANES, LANES), 0)
    books_ref[...] = jnp.zeros_like(books_ref)

    def tile(t, carry):
        i, j = t // tiles_across, t % tiles_across
        rows = pl.ds(pl.multiple_of(i * TILE_ROWS, TILE_ROWS), TILE_ROWS)
        codes = codes_ref[rows, pl.ds(pl.multiple_of(j * HALF, HALF), HALF)]
        left = grad_ref[rows, pl.ds(pl.multiple_of(j * TILE_COLS, LANES), LANES)]
        right = grad_ref[rows, pl.ds(pl.multiple_of(j * TILE_COLS + LANES, LANES), LANES)]
        even = jnp.where(first, pick(left, even_index), pick(right, even_index))
        odd = jnp.where(first, pick(left, even_index + 1), pick(right, even_index + 1))
        index = codes & (LANES - 1)
        upper = jnp.where(codes >= LANES, 1, 0)
        values, hots = [], []
        for n in range(TILE_ROWS):
            value = jnp.where(is_odd, odd[n : n + 1, :], even[n : n + 1, :])
            fits = is_upper == (jnp.broadcast_to(upper[n : n + 1, :], (8, LANES)) == 1)
            values.append(jnp.where(fits, value, 0.0))
            hots.append(jnp.where(entry == index[n : n + 1, :], 1.0, 0.0).astype(jnp.bfloat16))
        value = jnp.concatenate(values, axis=1)
        high = value.astype(jnp.bfloat16).astype(jnp.float32)
        parts = jnp.where(is_low, value - high, high).astype(jnp.bfloat16)
        sums = lax.dot_general(parts, jnp.concatenate(hots, axis=1), NT, preferred_element_type=jnp.float32)
        book = map_ref[i, j]
        books_ref[book] += sums[0:4, :] + sums[4:8, :]
        return carry

    lax.fori_loop(0, tiles_down * tiles_across, tile, 0, unroll=2)


def scatter(tile_map, codes, grad, books):
    total = pl.pallas_call(
        scatter_kernel,
        in_specs=[SMEM, VMEM, VMEM],
        out_specs=VMEM,
        out_shape=jax.ShapeDtypeStruct((books.shape[0] // 4, 4, LANES), jnp.float32),
        name="scatter",
    )(tile_map, codes, grad)
    return total.reshape(books.shape)


def update_kernel(n_row, n_col, grad_ref, books_ref, out_ref, col_in, row_sum, row_in, col_send, col_recv, row_send, row_recv, row_send2, row_recv2, col_send2, col_recv2):
    r, c = lax.axis_index("row"), lax.axis_index("col")
    wide = grad_ref.shape[0] // n_col
    thin = wide // n_row
    cols = [lax.rem(c + d, n_col) for d in range(n_col)]
    rows = [lax.rem(r + d, n_row) for d in range(n_row)]

    barrier = pltpu.get_barrier_semaphore()
    for d in range(1, n_col):
        pl.semaphore_signal(barrier, inc=1, device_id=(r, cols[d]), device_id_type=MESH)
    for d in range(1, n_row):
        pl.semaphore_signal(barrier, inc=1, device_id=(rows[d], c), device_id_type=MESH)
    pl.semaphore_wait(barrier, n_col + n_row - 2)

    def piece(index, size):
        return pl.ds(pl.multiple_of(index * size, size), size)

    def send(src, dst, sends, recvs, d, device):
        copy = pltpu.make_async_remote_copy(
            src_ref=src, dst_ref=dst, send_sem=sends.at[d], recv_sem=recvs.at[d], device_id=device, device_id_type=MESH
        )
        copy.start()
        return copy

    first = [
        send(grad_ref.at[piece(cols[d], wide)], col_in.at[d], col_send, col_recv, d, (r, cols[d])) for d in range(1, n_col)
    ]
    total = grad_ref[piece(c, wide), :]
    for d, copy in enumerate(first, 1):
        copy.wait_recv()
        total = total + col_in[d]
    row_sum[...] = total
    second = [
        send(row_sum.at[piece(rows[d], thin)], row_in.at[d], row_send, row_recv, d, (rows[d], c)) for d in range(1, n_row)
    ]
    total = row_sum[piece(r, thin), :]
    for d, copy in enumerate(second, 1):
        copy.wait_recv()
        total = total + row_in[d]
    mine = piece(c * n_row + r, thin)
    out_ref[mine, :] = books_ref[mine, :] - learn_rate * (2.0 * total)
    third = [send(out_ref.at[mine], out_ref.at[mine], row_send2, row_recv2, d, (rows[d], c)) for d in range(1, n_row)]
    for copy in third:
        copy.wait_recv()
    whole = piece(c, wide)
    fourth = [send(out_ref.at[whole], out_ref.at[whole], col_send2, col_recv2, d, (r, cols[d])) for d in range(1, n_col)]
    for copy in fourth:
        copy.wait_recv()
    for copy in first + second + third + fourth:
        copy.wait_send()


def update(n_row, n_col, grad, books):
    wide = books.shape[0] // n_col
    thin = wide // n_row
    dma = pltpu.SemaphoreType.DMA
    return pl.pallas_call(
        functools.partial(update_kernel, n_row, n_col),
        in_specs=[VMEM, VMEM],
        out_specs=VMEM,
        out_shape=jax.ShapeDtypeStruct(books.shape, jnp.float32),
        scratch_shapes=[
            pltpu.VMEM((n_col, wide, LANES), jnp.float32),
            pltpu.VMEM((wide, LANES), jnp.float32),
            pltpu.VMEM((n_row, thin, LANES), jnp.float32),
            dma((n_col,)),
            dma((n_col,)),
            dma((n_row,)),
            dma((n_row,)),
            dma((n_row,)),
            dma((n_row,)),
            dma((n_col,)),
            dma((n_col,)),
        ],
        compiler_params=pltpu.CompilerParams(collective_id=0, has_side_effects=True),
        name="update",
    )(grad, books)


def per_device(n_row, n_col, hessian, weights, codes, tile_map, codebooks):
    count, parts, entries = codebooks.shape
    books = codebooks.reshape(count, parts, entries // LANES, LANES).transpose(0, 2, 1, 3).reshape(-1, LANES)
    high, low = split_hessian(hessian)
    run = hessian.shape[2] * hessian.shape[3]
    maps = lax.all_gather(tile_map, ("row", "col"), axis=0)
    full_map = maps.reshape(n_row, n_col, *tile_map.shape).transpose(1, 2, 0, 3)
    full_map = full_map.reshape(n_col * tile_map.shape[0], n_row * tile_map.shape[1])
    error = errors(tile_map, codes, weights, books)
    piece = lax.all_to_all(error, "col", split_axis=1, concat_axis=0, tiled=True)
    piece, full_map, held_codes = lax.optimization_barrier((piece, full_map, codes))
    spread = lax.all_gather(piece, "row", axis=1, tiled=True)
    code_piece = lax.all_to_all(held_codes, "col", split_axis=1, concat_axis=0, tiled=True)
    code_spread = None
    for step in range(STEPS):
        grad = product(n_col, spread, high, low)
        if code_spread is None:
            grad, code_piece = lax.optimization_barrier((grad, code_piece))
            code_spread = lax.all_gather(code_piece, "row", axis=1, tiled=True)
        old, books = books, update(n_row, n_col, scatter(tile_map, codes, grad, books), books)
        if step < STEPS - 1:
            spread = shift(run, n_col * run, full_map, code_spread, spread, books, old)
    return books.reshape(count, entries // LANES, parts, LANES).transpose(0, 2, 1, 3).reshape(codebooks.shape)


def solution(mesh):
    placed = (P("row", None, "col", None), P("col", "row"), P("col", "row"), P("col", "row"), P())
    body = functools.partial(per_device, mesh.shape["row"], mesh.shape["col"])
    return jax.shard_map(body, mesh=mesh, in_specs=placed, out_specs=P(), check_vma=False)
```

```python
import functools

import jax
import jax.numpy as jnp
from jax import lax
from jax.experimental import pallas as pl
from jax.experimental.pallas import tpu as pltpu
from jax.sharding import PartitionSpec as P

TILE_ROWS = 16
TILE_COLS = 256
STEPS = 2
LANES = 128
HALF = TILE_COLS // 2

learn_rate = 0.01
MESH = pl.DeviceIdType.MESH
NT = (((1,), (1,)), ((), ()))


def split_kernel(hessian_ref, high_ref, low_ref):
    rows, width = high_ref.shape
    stride = width // LANES
    for k in range(stride):
        x = hessian_ref[pl.ds(k, rows, stride=stride), :]
        high = x.astype(jnp.bfloat16)
        high_ref[:, k * LANES : (k + 1) * LANES] = high
        low_ref[:, k * LANES : (k + 1) * LANES] = (x - high.astype(jnp.float32)).astype(jnp.bfloat16)


def split_hessian(hessian):
    rows = hessian.shape[0]
    width = hessian.shape[1] * hessian.shape[2] * hessian.shape[3]
    stride = width // LANES
    block = min(rows, 256)
    part = jax.ShapeDtypeStruct((rows, width), jnp.bfloat16)
    spec = pl.BlockSpec((block, width), lambda i: (i, 0))
    return pl.pallas_call(
        split_kernel,
        grid=(rows // block,),
        in_specs=[pl.BlockSpec((block * stride, LANES), lambda i: (i, 0))],
        out_specs=[spec, spec],
        out_shape=[part, part],
        cost_estimate=pl.CostEstimate(flops=rows * width * 4, bytes_accessed=rows * width * 8, transcendentals=0),
        name="split_hessian",
    )(hessian.reshape(rows * stride, LANES))


def pick(table, index):
    return jnp.take_along_axis(table, index, axis=1, mode="promise_in_bounds")


def lookup(table, code):
    index = code & (LANES - 1)
    upper = code >= LANES
    tables = [jnp.broadcast_to(table[n : n + 1, :], code.shape) for n in range(4)]
    even = jnp.where(upper, pick(tables[2], index), pick(tables[0], index))
    odd = jnp.where(upper, pick(tables[3], index), pick(tables[1], index))
    return even, odd


def error_kernel(map_ref, codes_ref, weights_ref, books_ref, error_ref):
    tiles_down, tiles_across = map_ref.shape
    lane = lax.broadcasted_iota(jnp.int32, (TILE_ROWS, LANES), 1)
    is_odd = (lane & 1) == 1

    def tile(t, carry):
        i, j = t // tiles_across, t % tiles_across
        rows = pl.ds(pl.multiple_of(i * TILE_ROWS, TILE_ROWS), TILE_ROWS)
        codes = codes_ref[rows, pl.ds(pl.multiple_of(j * HALF, HALF), HALF)]
        even, odd = lookup(books_ref[map_ref[i, j]], codes)
        for half in range(2):
            source = (lane >> 1) + half * (LANES // 2)
            value = jnp.where(is_odd, pick(odd, source), pick(even, source))
            columns = pl.ds(pl.multiple_of(j * TILE_COLS + half * LANES, LANES), LANES)
            error_ref[rows, columns] = value - weights_ref[rows, columns].astype(jnp.float32)
        return carry

    lax.fori_loop(0, tiles_down * tiles_across, tile, 0, unroll=4)


def shift_kernel(run, gap, col_ref, map_ref, codes_ref, error_ref, new_ref, old_ref, out_ref):
    rows_here, pairs = codes_ref.shape
    down, across = rows_here // TILE_ROWS, pairs // HALF
    top = pl.program_id(0) * down
    lane = lax.broadcasted_iota(jnp.int32, (TILE_ROWS, LANES), 1)
    is_odd = (lane & 1) == 1
    begin = col_ref[0] * run

    def table(i, column):
        place = (column // run) * gap + begin + column % run
        book = map_ref[top + i, place // TILE_COLS]
        return new_ref[book] - old_ref[book]

    def tile(t, carry):
        i, j = t // across, t % across
        rows = pl.ds(pl.multiple_of(i * TILE_ROWS, TILE_ROWS), TILE_ROWS)
        codes = codes_ref[rows, pl.ds(pl.multiple_of(j * HALF, HALF), HALF)]
        even, odd = lookup(table(i, j * TILE_COLS), codes)
        if run % TILE_COLS:
            even2, odd2 = lookup(table(i, j * TILE_COLS + LANES), codes)
            second = lane >= LANES // 2
            even, odd = jnp.where(second, even2, even), jnp.where(second, odd2, odd)
        for half in range(2):
            source = (lane >> 1) + half * (LANES // 2)
            value = jnp.where(is_odd, pick(odd, source), pick(even, source))
            columns = pl.ds(pl.multiple_of(j * TILE_COLS + half * LANES, LANES), LANES)
            out_ref[rows, columns] = error_ref[rows, columns] + value
        return carry

    lax.fori_loop(0, down * across, tile, 0, unroll=4)


def shift(run, gap, full_map, codes, error, new, old):
    m, k = error.shape
    block = min(m, 128)
    col = jnp.full((1,), lax.axis_index("col"), jnp.int32)
    books = pl.BlockSpec((new.shape[0] // 4, 4, LANES), lambda i: (0, 0, 0))
    spec = pl.BlockSpec((block, k), lambda i: (i, 0))
    return pl.pallas_call(
        functools.partial(shift_kernel, run, gap),
        grid=(m // block,),
        in_specs=[SMEM, SMEM, pl.BlockSpec((block, k // 2), lambda i: (i, 0)), spec, books, books],
        out_specs=spec,
        out_shape=jax.ShapeDtypeStruct((m, k), jnp.float32),
        name="shift",
    )(col, full_map, codes, error, new.reshape(-1, 4, LANES), old.reshape(-1, 4, LANES))


VMEM = pl.BlockSpec(memory_space=pltpu.VMEM)
SMEM = pl.BlockSpec(memory_space=pltpu.SMEM)


def errors(tile_map, codes, weights, books):
    return pl.pallas_call(
        error_kernel,
        in_specs=[SMEM, VMEM, VMEM, VMEM],
        out_specs=VMEM,
        out_shape=jax.ShapeDtypeStruct(weights.shape, jnp.float32),
        name="errors",
    )(tile_map, codes, weights, books.reshape(-1, 4, LANES))


def product_kernel(chunks, error_ref, high_ref, low_ref, out_ref, error_high, error_low, made, pair_in, pair_sum, chip_in, pair_send, pair_recv, chip_send, chip_recv):
    n = pl.program_id(0)
    r, c = lax.axis_index("row"), lax.axis_index("col")
    chips = made.shape[1]
    block = made.shape[4]
    chip, core = c // 2, lax.rem(c, 2)
    others = [lax.rem(chip + d, chips) for d in range(chips)]

    @pl.when(n == 0)
    def _():
        barrier = pltpu.get_barrier_semaphore()
        pl.semaphore_signal(barrier, inc=1, device_id=(r, chip * 2 + 1 - core), device_id_type=MESH)
        for d in range(1, chips):
            pl.semaphore_signal(barrier, inc=1, device_id=(r, others[d] * 2 + core), device_id_type=MESH)
        x = error_ref[...]
        high = x.astype(jnp.bfloat16)
        error_high[...] = high
        error_low[...] = (x - high.astype(jnp.float32)).astype(jnp.bfloat16)
        pl.semaphore_wait(barrier, chips)

    def to_pair(k):
        return pltpu.make_async_remote_copy(
            src_ref=made.at[k, :, 1 - core],
            dst_ref=pair_in.at[k],
            send_sem=pair_send.at[k],
            recv_sem=pair_recv.at[k],
            device_id=(r, chip * 2 + 1 - core),
            device_id_type=MESH,
        )

    def to_chip(k, d):
        return pltpu.make_async_remote_copy(
            src_ref=pair_sum.at[k, others[d]],
            dst_ref=chip_in.at[d - 1, k],
            send_sem=chip_send.at[d - 1, k],
            recv_sem=chip_recv.at[d - 1, k],
            device_id=(r, others[d] * 2 + core),
            device_id_type=MESH,
        )

    def add_pair(k):
        to_pair(k).wait_recv()
        pair_sum[k] = made[k, :, core] + pair_in[k]
        for d in range(1, chips):
            to_chip(k, d).start()

    dot = functools.partial(lax.dot_general, dimension_numbers=NT, preferred_element_type=jnp.float32)
    total = dot(error_high[...], low_ref[...]) + dot(error_low[...], high_ref[...])
    total = total + dot(error_high[...], high_ref[...])
    made[n] = total.reshape(made.shape[1:])
    to_pair(n).start()

    @pl.when(n > 0)
    def _():
        add_pair(n - 1)

    @pl.when(n == chunks - 1)
    def _():
        add_pair(n)

        def finish(k, carry):
            total = pair_sum[k, chip]
            for d in range(1, chips):
                to_chip(k, d).wait_recv()
                total = total + chip_in[d - 1, k]
            out_ref[:, pl.ds(pl.multiple_of(k * block, block), block)] = total
            to_pair(k).wait_send()
            for d in range(1, chips):
                to_chip(k, d).wait_send()
            return carry

        lax.fori_loop(0, chunks, finish, 0)


def product(n_col, error, high, low):
    m, k = error.shape
    n = high.shape[0]
    block = min(n, 512)
    chunks = n // block
    chips = n_col // 2
    rows = m // n_col
    spec = pl.BlockSpec((block, k), lambda i: (i, 0))
    dma = pltpu.SemaphoreType.DMA
    return pl.pallas_call(
        functools.partial(product_kernel, chunks),
        grid=(chunks,),
        in_specs=[pl.BlockSpec((m, k), lambda i: (0, 0)), spec, spec],
        out_specs=pl.BlockSpec((rows, n), lambda i: (0, 0)),
        out_shape=jax.ShapeDtypeStruct((rows, n), jnp.float32),
        scratch_shapes=[
            pltpu.VMEM((m, k), jnp.bfloat16),
            pltpu.VMEM((m, k), jnp.bfloat16),
            pltpu.VMEM((chunks, chips, 2, rows, block), jnp.float32),
            pltpu.VMEM((chunks, chips, rows, block), jnp.float32),
            pltpu.VMEM((chunks, chips, rows, block), jnp.float32),
            pltpu.VMEM((chips - 1, chunks, rows, block), jnp.float32),
            dma((chunks,)),
            dma((chunks,)),
            dma((chips - 1, chunks)),
            dma((chips - 1, chunks)),
        ],
        compiler_params=pltpu.CompilerParams(collective_id=1, has_side_effects=True, vmem_limit_bytes=56 * 2**20),
        cost_estimate=pl.CostEstimate(flops=6 * m * n * k, bytes_accessed=4 * n * k + 4 * m * (n + k), transcendentals=0),
        name="product",
    )(error, high, low)


def scatter_kernel(map_ref, codes_ref, grad_ref, books_ref):
    tiles_down, tiles_across = map_ref.shape
    shape = (TILE_ROWS, LANES)
    lane = lax.broadcasted_iota(jnp.int32, shape, 1)
    first = lane < LANES // 2
    even_index = (2 * lane) & (LANES - 1)
    line = lax.broadcasted_iota(jnp.int32, (8, LANES), 0)
    is_odd = (line & 1) == 1
    is_upper = (line & 2) == 2
    is_low = lax.broadcasted_iota(jnp.int32, (8, HALF * TILE_ROWS), 0) >= 4
    entry = lax.broadcasted_iota(jnp.int32, (LANES, LANES), 0)
    books_ref[...] = jnp.zeros_like(books_ref)

    def tile(t, carry):
        i, j = t // tiles_across, t % tiles_across
        rows = pl.ds(pl.multiple_of(i * TILE_ROWS, TILE_ROWS), TILE_ROWS)
        codes = codes_ref[rows, pl.ds(pl.multiple_of(j * HALF, HALF), HALF)]
        left = grad_ref[rows, pl.ds(pl.multiple_of(j * TILE_COLS, LANES), LANES)]
        right = grad_ref[rows, pl.ds(pl.multiple_of(j * TILE_COLS + LANES, LANES), LANES)]
        even = jnp.where(first, pick(left, even_index), pick(right, even_index))
        odd = jnp.where(first, pick(left, even_index + 1), pick(right, even_index + 1))
        index = codes & (LANES - 1)
        upper = jnp.where(codes >= LANES, 1, 0)
        values, hots = [], []
        for n in range(TILE_ROWS):
            value = jnp.where(is_odd, odd[n : n + 1, :], even[n : n + 1, :])
            fits = is_upper == (jnp.broadcast_to(upper[n : n + 1, :], (8, LANES)) == 1)
            values.append(jnp.where(fits, value, 0.0))
            hots.append(jnp.where(entry == index[n : n + 1, :], 1.0, 0.0).astype(jnp.bfloat16))
        value = jnp.concatenate(values, axis=1)
        high = value.astype(jnp.bfloat16).astype(jnp.float32)
        parts = jnp.where(is_low, value - high, high).astype(jnp.bfloat16)
        sums = lax.dot_general(parts, jnp.concatenate(hots, axis=1), NT, preferred_element_type=jnp.float32)
        book = map_ref[i, j]
        books_ref[book] += sums[0:4, :] + sums[4:8, :]
        return carry

    lax.fori_loop(0, tiles_down * tiles_across, tile, 0, unroll=2)


def scatter(tile_map, codes, grad, books):
    total = pl.pallas_call(
        scatter_kernel,
        in_specs=[SMEM, VMEM, VMEM],
        out_specs=VMEM,
        out_shape=jax.ShapeDtypeStruct((books.shape[0] // 4, 4, LANES), jnp.float32),
        name="scatter",
    )(tile_map, codes, grad)
    return total.reshape(books.shape)


def update_kernel(n_row, n_col, grad_ref, books_ref, map_ref, out_ref, maps_ref, col_in, row_sum, row_in, col_send, col_recv, row_send, row_recv, row_send2, row_recv2, col_send2, col_recv2, map_send, map_recv, map_send2, map_recv2):
    r, c = lax.axis_index("row"), lax.axis_index("col")
    wide = grad_ref.shape[0] // n_col
    thin = wide // n_row
    cols = [lax.rem(c + d, n_col) for d in range(n_col)]
    rows = [lax.rem(r + d, n_row) for d in range(n_row)]

    barrier = pltpu.get_barrier_semaphore()
    for d in range(1, n_col):
        pl.semaphore_signal(barrier, inc=1, device_id=(r, cols[d]), device_id_type=MESH)
    for d in range(1, n_row):
        pl.semaphore_signal(barrier, inc=1, device_id=(rows[d], c), device_id_type=MESH)
    pl.semaphore_wait(barrier, n_col + n_row - 2)

    def piece(index, size):
        return pl.ds(pl.multiple_of(index * size, size), size)

    def send(src, dst, sends, recvs, d, device):
        copy = pltpu.make_async_remote_copy(
            src_ref=src, dst_ref=dst, send_sem=sends.at[d], recv_sem=recvs.at[d], device_id=device, device_id_type=MESH
        )
        copy.start()
        return copy

    first = [
        send(grad_ref.at[piece(cols[d], wide)], col_in.at[d], col_send, col_recv, d, (r, cols[d])) for d in range(1, n_col)
    ]
    maps = [send(map_ref, maps_ref.at[r, c], map_send, map_recv, d, (r, cols[d])) for d in range(1, n_col)]
    maps_ref[r, c] = map_ref[...]
    total = grad_ref[piece(c, wide), :]
    for d, copy in enumerate(first, 1):
        copy.wait_recv()
        total = total + col_in[d]
    row_sum[...] = total
    second = [
        send(row_sum.at[piece(rows[d], thin)], row_in.at[d], row_send, row_recv, d, (rows[d], c)) for d in range(1, n_row)
    ]
    for copy in maps:
        copy.wait_recv()
    lines = [send(maps_ref.at[r], maps_ref.at[r], map_send2, map_recv2, d, (rows[d], c)) for d in range(1, n_row)]
    total = row_sum[piece(r, thin), :]
    for d, copy in enumerate(second, 1):
        copy.wait_recv()
        total = total + row_in[d]
    mine = piece(c * n_row + r, thin)
    out_ref[mine, :] = books_ref[mine, :] - learn_rate * (2.0 * total)
    third = [send(out_ref.at[mine], out_ref.at[mine], row_send2, row_recv2, d, (rows[d], c)) for d in range(1, n_row)]
    for copy in third:
        copy.wait_recv()
    whole = piece(c, wide)
    fourth = [send(out_ref.at[whole], out_ref.at[whole], col_send2, col_recv2, d, (r, cols[d])) for d in range(1, n_col)]
    for copy in fourth:
        copy.wait_recv()
    for copy in lines:
        copy.wait_recv()
    for copy in first + second + third + fourth + maps + lines:
        copy.wait_send()


def update(n_row, n_col, grad, books, padded):
    wide = books.shape[0] // n_col
    thin = wide // n_row
    dma = pltpu.SemaphoreType.DMA
    return pl.pallas_call(
        functools.partial(update_kernel, n_row, n_col),
        in_specs=[VMEM, VMEM, VMEM],
        out_specs=[VMEM, VMEM],
        out_shape=[
            jax.ShapeDtypeStruct(books.shape, jnp.float32),
            jax.ShapeDtypeStruct((n_row, n_col) + padded.shape, jnp.int32),
        ],
        scratch_shapes=[
            pltpu.VMEM((n_col, wide, LANES), jnp.float32),
            pltpu.VMEM((wide, LANES), jnp.float32),
            pltpu.VMEM((n_row, thin, LANES), jnp.float32),
            dma((n_col,)),
            dma((n_col,)),
            dma((n_row,)),
            dma((n_row,)),
            dma((n_row,)),
            dma((n_row,)),
            dma((n_col,)),
            dma((n_col,)),
            dma((n_col,)),
            dma((n_col,)),
            dma((n_row,)),
            dma((n_row,)),
        ],
        compiler_params=pltpu.CompilerParams(collective_id=0, has_side_effects=True),
        name="update",
    )(grad, books, padded)


def per_device(n_row, n_col, hessian, weights, codes, tile_map, codebooks):
    count, parts, entries = codebooks.shape
    books = codebooks.reshape(count, parts, entries // LANES, LANES).transpose(0, 2, 1, 3).reshape(-1, LANES)
    high, low = split_hessian(hessian)
    run = hessian.shape[2] * hessian.shape[3]
    down, across = tile_map.shape
    padded = jnp.pad(tile_map, ((0, -down % 8), (0, -across % LANES)))
    error = errors(tile_map, codes, weights, books)
    piece = lax.all_to_all(error, "col", split_axis=1, concat_axis=0, tiled=True)
    piece, held_codes = lax.optimization_barrier((piece, codes))
    spread = lax.all_gather(piece, "row", axis=1, tiled=True)
    code_piece = lax.all_to_all(held_codes, "col", split_axis=1, concat_axis=0, tiled=True)
    code_spread = None
    for step in range(STEPS):
        grad = product(n_col, spread, high, low)
        if code_spread is None:
            grad, code_piece = lax.optimization_barrier((grad, code_piece))
            code_spread = lax.all_gather(code_piece, "row", axis=1, tiled=True)
        old = books
        books, maps = update(n_row, n_col, scatter(tile_map, codes, grad, books), books, padded)
        if step < STEPS - 1:
            full_map = maps[:, :, :down, :across].transpose(1, 2, 0, 3).reshape(n_col * down, n_row * across)
            spread = shift(run, n_col * run, full_map, code_spread, spread, books, old)
    return books.reshape(count, entries // LANES, parts, LANES).transpose(0, 2, 1, 3).reshape(codebooks.shape)


def solution(mesh):
    placed = (P("row", None, "col", None), P("col", "row"), P("col", "row"), P("col", "row"), P())
    body = functools.partial(per_device, mesh.shape["row"], mesh.shape["col"])
    return jax.shard_map(body, mesh=mesh, in_specs=placed, out_specs=P(), check_vma=False)
```
